32 devices in a mesh: row: 8 (over z, core), col: 4 (over y, x).
Axes of the slice: x: 2, y: 2, z: 4, core: 2. Of those that a mesh axis runs over, the one named last changes fastest.
Arguments:
- gram: bfloat16 [16384, 16384], P('row', 'col'), as said below
- corr: float32 [16384, 128], P('row'), may hold values from -6 to 6
- beta_start: float32 [16384, 2, 128], P('col'), may hold values from -4 to 4
- lambdas: float32 [2], replicated, may hold values from 0.2 to 0.8
- penalty: float32 [262144], replicated, may hold values from 0.5 to 2
- strong: int32 [16384], P('row'), may hold values from 0 to 262143
- active: int32 [2, 8], replicated, may hold values 0 or 1
- order: int32 [8], replicated, may hold values from 0 to 7, each once
Outputs:
- beta: float32 [16384, 2, 128], P('col')
- grad: float32 [16384, 2, 128], P('row')
The draws below stay inside these ranges and needn't reach their ends.
Inputs may be any that keep to these rules, and one draw needn't show every extreme that they name: `order`: a permutation of the block numbers. `gram`: symmetric, positive definite, diagonal entries of order one.
All inputs are finite; a program needn't handle non-finite values.
Results may differ from the reference program's by a relative error of at most 0.0046.
Values may be sent and summed in bfloat16 or wider, within the bound.
No kernel may reach another device: no remote copies, remote signals or barrier semaphores. Data moves between devices by JAX's collectives and lax.ppermute only.
A program may use at most 128 MiB of HBM per device.

```python
import math
import jax
import jax.numpy as jnp
from jax import lax

BW = 2048
RESP = 128
NL = 2
VARIANTS = 262144
NB = 8
P_SIZE = 16384


def draw_gram(key, part):
    key_off, key_diag = jax.random.split(key)
    base = jax.random.normal(key_off, (P_SIZE, P_SIZE), jnp.float32)
    off_part = (base + base.T) * (0.35 / math.sqrt(P_SIZE))
    diag_part = jax.random.uniform(key_diag, (P_SIZE,), jnp.float32, 1.2, 2.4)
    row_ids = lax.broadcasted_iota(jnp.int32, (P_SIZE, P_SIZE), 0)
    col_ids = lax.broadcasted_iota(jnp.int32, (P_SIZE, P_SIZE), 1)
    return jnp.where(row_ids == col_ids, diag_part[:, None], off_part).astype(jnp.bfloat16)


def touch_ends(array, own_key, least, top_value):
    longest = array.shape.index(max(array.shape))
    spots = []
    for shift in (0, 1):
        where = [jax.random.randint(jax.random.fold_in(own_key, axis), (), 0, length) for axis, length in enumerate(array.shape)]
        where[longest] = (where[longest] + shift) % array.shape[longest]
        spots.append(tuple(where))
    return array.at[spots[0]].set(least).at[spots[1]].set(top_value)


def level_of(key, shape, pieces, smallest, high):
    def one(dim, shards_of):
        steps = jax.random.uniform(jax.random.fold_in(jax.random.fold_in(key, 6), dim), (shards_of,), jnp.float32, smallest / len(pieces), high / len(pieces))
        return jnp.repeat(jnp.exp(steps), shape[dim] // shards_of).reshape((-1,) + (1,) * (len(shape) - dim - 1))

    level = one(*pieces[0])
    for cut in pieces[1:]:
        level = level * one(*cut)
    return level


def gaussian(key, extent, spread, bound, shards=(), dtype=jnp.bfloat16):
    loudness = level_of(key, extent, shards, -0.22, 0.18) if shards else 1.0
    array = jax.random.normal(key, extent, jnp.float32) * spread * loudness
    return jnp.minimum(jnp.maximum(array, -bound), bound).astype(dtype)


def setup_inputs(seed: int = 0) -> dict:
    keys = jax.random.split(jax.random.key(seed), 9)
    gram = draw_gram(jax.random.fold_in(keys[8], 71), 0)
    corr = gaussian(keys[1], (P_SIZE, RESP), 1.0, 6.0, ((0, 8),), jnp.float32)
    beta_start = gaussian(keys[2], (P_SIZE, NL, RESP), 0.3, 4.0, ((0, 4),), jnp.float32)
    lambdas = jnp.clip(jnp.exp(jax.random.uniform(keys[3], (NL,), jnp.float32, math.log(0.2), math.log(0.8))), 0.2, 0.8)
    penalty = jnp.clip(jnp.exp(jax.random.uniform(keys[4], (VARIANTS,), jnp.float32, math.log(0.5), math.log(2.0))), 0.5, 2.0)
    strong = touch_ends(jax.random.randint(keys[5], (P_SIZE,), 0, VARIANTS), jax.random.fold_in(keys[5], 1), 0, VARIANTS - 1).astype(jnp.int32)
    active = touch_ends((jax.random.randint(keys[6], (NL, NB), 0, 4) < 3).astype(jnp.int32), jax.random.fold_in(keys[6], 1), 0, 1)
    order = jax.random.permutation(keys[7], NB).astype(jnp.int32)
    return {"gram": gram, "corr": corr, "beta_start": beta_start, "lambdas": lambdas, "penalty": penalty, "strong": strong, "active": active, "order": order}


def reference(gram, corr, beta_start, lambdas, penalty, strong, active, order):
    full_rows = gram.shape[0]
    lam_count = beta_start.shape[1]
    phenos = beta_start.shape[2]
    diag_gram = jnp.diagonal(gram).astype(jnp.float32)
    thresh = lambdas[None, :] * penalty[strong][:, None]
    beta_round = beta_start.astype(jnp.bfloat16).reshape(full_rows, lam_count * phenos)
    product = jnp.dot(gram, beta_round, preferred_element_type=jnp.float32)
    grad = corr[:, None, :] - product.reshape(full_rows, lam_count, phenos)
    beta = beta_start

    def visit(turn, carry):
        beta, grad = carry
        block = order[turn]
        start = (block * BW).astype(jnp.int32)
        beta_old = lax.dynamic_slice_in_dim(beta, start, BW, 0)
        grad_now = lax.dynamic_slice_in_dim(grad, start, BW, 0)
        diag_now = lax.dynamic_slice_in_dim(diag_gram, start, BW, 0)[:, None, None]
        thresh_now = lax.dynamic_slice_in_dim(thresh, start, BW, 0)[:, :, None]
        shifted = diag_now * beta_old + grad_now
        beta_new = jnp.sign(shifted) * jnp.maximum(jnp.abs(shifted) - thresh_now, 0.0) / diag_now
        active_now = lax.dynamic_index_in_dim(active, block, 1, keepdims=False)
        beta_new = jnp.where(active_now[None, :, None] == 1, beta_new, beta_old)
        step_bf = (beta_new - beta_old).astype(jnp.bfloat16)
        beta = lax.dynamic_update_slice_in_dim(beta, beta_old + step_bf.astype(jnp.float32), start, 0)
        gram_cols = lax.dynamic_slice_in_dim(gram, start, BW, 1)
        change = jnp.dot(gram_cols, step_bf.reshape(BW, lam_count * phenos), preferred_element_type=jnp.float32).astype(jnp.bfloat16)
        grad = grad - change.astype(jnp.float32).reshape(full_rows, lam_count, phenos)
        return beta, grad

    beta, grad = lax.fori_loop(0, order.shape[0], visit, (beta, grad))
    return beta, grad
```

```python
import functools

import jax
import jax.numpy as jnp
import numpy as np
from jax import lax
from jax.experimental import pallas as pl
from jax.experimental.pallas import tpu as pltpu
from jax.sharding import PartitionSpec as P

NT = (((1,), (1,)), ((), ()))


def device_pairs(flows, planes, lines):
    nxt = dict(flows)
    for start in [a for a in nxt if a not in nxt.values()]:
        end = start
        while end in nxt:
            end = nxt[end]
        nxt[end] = start
    pairs = []
    for z in range(planes):
        for q in range(lines):
            for k in range(2):
                to_z, to_q = nxt.get((z, q), (z, q))
                to_k = k if (z, q) in nxt else 1 - k
                pairs.append(((2 * z + k) * lines + q, (2 * to_z + to_k) * lines + to_q))
    return pairs


def step_kernel(s_ref, lam_ref, act_ref, pen_ref, diag_ref, beta_ref, grad_ref, acc_ref, next_ref, *rest):
    *got, step_ref, pay_ref = rest
    beta_old, diag = beta_ref[0], diag_ref[0]
    grad = grad_ref[0] - acc_ref[0]
    for r in got:
        grad = grad - r[...].astype(jnp.float32)
    shifted = diag * beta_old + grad
    size = jnp.maximum(jnp.abs(shifted) - lam_ref[...] * pen_ref[0], 0.0) / diag
    beta_new = jnp.where(shifted < 0.0, -size, size)
    step = jnp.where(act_ref[0] == 1, beta_new - beta_old, 0.0).astype(jnp.bfloat16)
    step_ref[...] = step

    @pl.when(s_ref[3] == 1)
    def _():
        pay_ref[...] = step

    @pl.when(s_ref[3] == 0)
    def _():
        pay_ref[...] = next_ref[0].astype(pay_ref.dtype)


def soft_step(scalars, lam, act, pen, diag, beta, grad, acc, got, tile=512):
    _, resp, width = beta.shape
    column = pl.BlockSpec((resp, 1), lambda i, s: (0, 0))
    line = pl.BlockSpec((1, 1, tile), lambda i, s: (s[0], 0, i))
    now = pl.BlockSpec((1, resp, tile), lambda i, s: (s[0], 0, i))
    after = pl.BlockSpec((1, resp, tile), lambda i, s: (s[2], 0, i))
    flat = pl.BlockSpec((resp, tile), lambda i, s: (0, i))
    return pl.pallas_call(
        step_kernel,
        grid_spec=pltpu.PrefetchScalarGridSpec(
            num_scalar_prefetch=1,
            grid=(width // tile,),
            in_specs=[column, pl.BlockSpec((1, resp, 1), lambda i, s: (s[1], 0, 0)), line, line, now, now, now, after]
            + [flat] * len(got),
            out_specs=[flat, flat],
        ),
        out_shape=[jax.ShapeDtypeStruct((resp, width), jnp.bfloat16)] * 2,
        compiler_params=pltpu.CompilerParams(dimension_semantics=("arbitrary",)),
        cost_estimate=pl.CostEstimate(flops=20 * resp * width, bytes_accessed=22 * resp * width, transcendentals=0),
    )(scalars, lam, act, pen, diag, beta, grad, acc, acc, *got)


def times_block(x, own, own_ref, sib_ref):
    block = jnp.where(own == 1, own_ref[...], sib_ref[...])
    change = lax.dot_general(x, block, NT, preferred_element_type=jnp.float32)
    return change.astype(jnp.bfloat16).astype(jnp.float32)


def relay_kernel(s_ref, x_ref, step_ref, own_ref, sib_ref, acc_ref, send_ref, *, tile):
    i = pl.program_id(0)

    @pl.when(s_ref[0] == 1)
    def _():
        total = acc_ref[0] + times_block(x_ref[...], s_ref[2], own_ref, sib_ref)
        send_ref[...] = total.astype(send_ref.dtype)

    @pl.when(s_ref[0] == 0)
    def _():
        send_ref[...] = step_ref[...]


def relay(scalars, x, step, g_own, g_sib, acc, tile=512):
    resp, width = x.shape
    flat = pl.BlockSpec((resp, tile), lambda i, s: (0, i))
    return pl.pallas_call(
        functools.partial(relay_kernel, tile=tile),
        grid_spec=pltpu.PrefetchScalarGridSpec(
            num_scalar_prefetch=1,
            grid=(width // tile,),
            in_specs=[
                pl.BlockSpec((resp, width), lambda i, s: (0, 0)),
                flat,
                pl.BlockSpec((tile, width), lambda i, s: (i * s[0] * s[2], s[3])),
                pl.BlockSpec((tile, width), lambda i, s: (i * s[0] * (1 - s[2]), s[3])),
                pl.BlockSpec((1, resp, tile), lambda i, s: (s[1], 0, i)),
            ],
            out_specs=flat,
        ),
        out_shape=jax.ShapeDtypeStruct((resp, width), jnp.bfloat16),
        compiler_params=pltpu.CompilerParams(dimension_semantics=("arbitrary",), vmem_limit_bytes=32 << 20),
        cost_estimate=pl.CostEstimate(
            flops=2 * resp * width * width, bytes_accessed=2 * width * width, transcendentals=0
        ),
    )(scalars, x, step, g_own, g_sib, acc)


def update_kernel(s_ref, own_ref, sib_ref, acc_ref, moved_ref, *rest):
    *arrived, out_ref, moved_out, x_ref = rest
    j, i = pl.program_id(0), pl.program_id(1)
    live, own = s_ref[0], 1 - (s_ref[1] ^ j)

    @pl.when((i == 0) & (j == 0))
    def _():
        for n, r in enumerate(arrived):
            @pl.when(s_ref[3] == n)
            def _():
                x_ref[...] = r[...]

        @pl.when(live == 1)
        def _():
            moved_out[0] = x_ref[...]

        @pl.when(live == 0)
        def _():
            moved_out[0] = moved_ref[0]

    @pl.when(live == 1)
    def _():
        out_ref[0] = acc_ref[0] + times_block(x_ref[...], own, own_ref, sib_ref)

    @pl.when(live == 0)
    def _():
        out_ref[0] = acc_ref[0]


def update(scalars, g_own, g_sib, acc, moved, arrived, tile=512):
    _, resp, width = acc.shape
    acc_spec = pl.BlockSpec((1, resp, tile), lambda j, i, s: (j, 0, i))
    moved_spec = pl.BlockSpec((1, resp, width), lambda j, i, s: (s[2], 0, 0))
    full = pl.BlockSpec((resp, width), lambda j, i, s: (0, 0))
    return pl.pallas_call(
        update_kernel,
        grid_spec=pltpu.PrefetchScalarGridSpec(
            num_scalar_prefetch=1,
            grid=(2, width // tile),
            in_specs=[
                pl.BlockSpec((tile, width), lambda j, i, s: (i * s[0] * (1 - (s[1] ^ j)), s[2])),
                pl.BlockSpec((tile, width), lambda j, i, s: (i * s[0] * (s[1] ^ j), s[2])),
                acc_spec,
                moved_spec,
            ] + [full] * len(arrived),
            out_specs=[acc_spec, moved_spec],
            scratch_shapes=[pltpu.VMEM((resp, width), jnp.bfloat16)],
        ),
        out_shape=[jax.ShapeDtypeStruct(acc.shape, acc.dtype), jax.ShapeDtypeStruct(moved.shape, moved.dtype)],
        input_output_aliases={3: 0, 4: 1},
        compiler_params=pltpu.CompilerParams(
            dimension_semantics=("arbitrary", "arbitrary"), vmem_limit_bytes=40 << 20
        ),
        cost_estimate=pl.CostEstimate(
            flops=4 * resp * width * width, bytes_accessed=4 * width * width, transcendentals=0
        ),
    )(scalars, g_own, g_sib, acc, moved, *arrived)


def per_device(planes, lines, gram, corr, beta_start, lambdas, penalty, strong, active, order):
    width = corr.shape[0]
    lam_count, phenos = beta_start.shape[1:]
    cols = lam_count * phenos
    half = cols // 2
    row = lax.axis_index("row")
    z, k, q = row // 2, row % 2, lax.axis_index("col")
    swap = [(r * lines + c, (r ^ 1) * lines + c) for r in range(2 * planes) for c in range(lines)]
    permute = lambda x, pairs: lax.ppermute(x, ("row", "col"), pairs)
    ordered = lambda mine, other: jnp.where(k == 0, jnp.stack([mine, other]), jnp.stack([other, mine]))

    def gather_col(x):
        return lax.all_to_all(jnp.broadcast_to(x[None], (lines, *x.shape)), "col", 0, 0)

    g_sib = permute(gram, swap)

    fine = 128
    wanted = penalty.reshape(-1, fine)[strong // fine]
    pen_own = jnp.sum(jnp.where(lax.broadcasted_iota(jnp.int32, wanted.shape, 1) == (strong % fine)[:, None], wanted, 0.0), axis=1)
    tiles = width // fine
    slot = lax.dynamic_slice_in_dim(gram, k * width, width, 1)
    square = jnp.stack([slot[i * fine : (i + 1) * fine, i * fine : (i + 1) * fine] for i in range(tiles)])
    diag_own = jnp.sum(jnp.where(jnp.eye(fine, dtype=bool)[None], square.astype(jnp.float32), 0.0), axis=1).reshape(width)
    small_own = jnp.stack([pen_own, diag_own])
    small = ordered(small_own, permute(small_own, swap))
    pen, diag = small[:, :1], small[:, 1:]

    flat = beta_start.reshape(2 * width, cols)
    product = jnp.dot(gram, flat.astype(jnp.bfloat16), preferred_element_type=jnp.float32).T
    shares = lax.all_to_all(product.reshape(lines, cols // lines, width), "col", 0, 0)
    summed = gather_col(jnp.sum(shares, axis=0)).reshape(cols, width)
    grad_own = jnp.tile(corr.T, (lam_count, 1)) - summed
    grad_half = grad_own.reshape(2, half, width)
    mine = lax.dynamic_index_in_dim(grad_half, k, 0, keepdims=False)
    other = permute(lax.dynamic_index_in_dim(grad_half, 1 - k, 0, keepdims=False), swap)
    grad0 = ordered(mine, other)

    beta_half = lax.dynamic_slice_in_dim(flat, k * half, half, 1).reshape(2, width, half)
    beta0 = jnp.swapaxes(beta_half, 1, 2)
    lam = lax.dynamic_slice_in_dim(jnp.repeat(lambdas, phenos), k * half, half)[:, None]
    act = lax.dynamic_slice_in_dim(jnp.repeat(active.T, phenos, axis=1), k * half, half, 1)[:, :, None]
    flag = lambda v: v.astype(jnp.int32)

    def routes(p, pn):
        rest_q = [c for c in range(lines) if c not in (p, pn)]
        rest_z = sorted([c for c in range(planes) if c not in (p, pn)], key=lambda c: abs(c - p) - abs(c - pn))
        if p == pn:
            return [([((p, p), (c, p)), ((p, c), (p, p))], c, p) for c in rest_z]
        first = ([((p, p), (pn, p))] + [((pn, c), (pn, pn)) for c in rest_q[:1]], pn, p)
        last = ([((pn, p), (pn, pn))] + [((p, p), (c, p)) for c in rest_z[:1]], rest_z[0] if rest_z else pn, p)
        between = []
        for line, plane in zip(rest_q[1:], rest_z[1:]):
            source = p if abs(plane - p) <= abs(plane - pn) else pn
            between.append(([((source, p), (plane, p)), ((pn, line), (pn, pn))], plane, source))
        return [first, *between, last]

    holds = np.zeros((planes, planes, planes), np.int32)
    for p in range(planes):
        for pn in range(planes):
            for n, (_, plane, _) in enumerate(routes(p, pn)):
                holds[p, pn, plane] = n + 1
            holds[p, pn, p] = 0

    def branch(p, pn):
        plan = routes(p, pn)
        send = lambda payload, flows: permute(payload, device_pairs(flows, planes, lines))

        def run(operands):
            step, pay, acc, g_own, g_sib, s, sn = operands
            if p == pn:
                return tuple(send(pay, flows) for flows, _, _ in plan)
            at_pn = (z == pn) & (q == p)
            first = send(pay, plan[0][0])
            scalars = jnp.stack([flag(at_pn), sn, flag(k == sn), s])
            out = relay(scalars, first, step, g_own, g_sib, acc)
            between = [
                send(pay if source == p else jnp.where(at_pn, first, pay), flows) for flows, _, source in plan[1:-1]
            ]
            return (first, *between, send(out, plan[-1][0]))

        return run

    branches = [branch(p, pn) for p in range(planes) for pn in range(planes)]
    visits = order.shape[0]

    def visit(turn, carry):
        acc, moved, got = carry
        block = order[turn]
        after = order[jnp.minimum(turn + 1, visits - 1)]
        p, s, pn, sn = block // 2, block % 2, after // 2, after % 2
        live = flag(q == p)
        scalars = jnp.stack([s, block, sn, flag((z == p) & (q == p))])
        step, pay = soft_step(scalars, lam, act, pen, diag, beta0, grad0, acc, got)
        got = lax.switch(p * planes + pn, branches, (step, pay, acc, gram, g_sib, s, sn))
        scalars = jnp.stack([live, k, s, jnp.asarray(holds)[p, pn, z]])
        acc, moved = update(scalars, gram, g_sib, acc, moved, (step, *got))
        return acc, moved, got

    zero = jnp.zeros((2, half, width), jnp.float32)
    small_zero = zero.astype(jnp.bfloat16)
    acc, moved, _ = lax.fori_loop(0, visits, visit, (zero, small_zero, (small_zero[0],) * (planes - 1)))

    moved_all = ordered(moved, permute(moved, swap))
    moved_all = moved_all.transpose(1, 3, 0, 2).reshape(2 * width, cols)
    beta = (flat + moved_all.astype(jnp.float32)).reshape(beta_start.shape)

    share = acc.astype(jnp.bfloat16).reshape(2, lines, half // lines, width).swapaxes(0, 1)
    share = jnp.sum(lax.all_to_all(share, "col", 0, 0).astype(jnp.float32), axis=0)
    at = lax.axis_index("col") * (half // lines)
    share = (lax.dynamic_slice_in_dim(grad0, at, half // lines, 1) - share).astype(jnp.bfloat16)
    final = gather_col(share).swapaxes(0, 1).reshape(2, half, width)
    mine = lax.dynamic_index_in_dim(final, k, 0, keepdims=False)
    other = permute(lax.dynamic_index_in_dim(final, 1 - k, 0, keepdims=False), swap)
    final = ordered(mine, other).reshape(cols, width)
    grad = final.T.reshape(width, lam_count, phenos).astype(jnp.float32)
    return beta, grad


def solution(mesh):
    planes, lines = mesh.shape["row"] // 2, mesh.shape["col"]
    in_specs = (P("row", "col"), P("row", None), P("col", None, None), P(), P(), P("row"), P(), P())
    out_specs = (P("col", None, None), P("row", None, None))
    return jax.shard_map(
        functools.partial(per_device, planes, lines),
        mesh=mesh, in_specs=in_specs, out_specs=out_specs, check_vma=False,
    )
```

```python
import functools

import jax
import jax.numpy as jnp
import numpy as np
from jax import lax
from jax.experimental import pallas as pl
from jax.experimental.pallas import tpu as pltpu
from jax.sharding import PartitionSpec as P

FIELDS = 9
SLOT, BLOCK, PLACE, VISITED, LINE, HOLDS, RELAYS, NEXT, SENDS = range(FIELDS)


def flag(value):
    return value.astype(jnp.int32)


def at(turn, table, field):
    return table[turn[0] * FIELDS + field]


def device_pairs(flows, planes, lines):
    nxt = dict(flows)
    for start in [a for a in nxt if a not in nxt.values()]:
        end = start
        while end in nxt:
            end = nxt[end]
        nxt[end] = start
    pairs = []
    for z in range(planes):
        for q in range(lines):
            for k in range(2):
                to_z, to_q = nxt.get((z, q), (z, q))
                to_k = k if (z, q) in nxt else 1 - k
                pairs.append(((2 * z + k) * lines + q, (2 * to_z + to_k) * lines + to_q))
    return pairs


def diag_kernel(s_ref, block_ref, out_ref):
    rows = lax.broadcasted_iota(jnp.int32, block_ref.shape, 0)
    cols = lax.broadcasted_iota(jnp.int32, block_ref.shape, 1)
    kept = jnp.where(rows == cols, block_ref[...].astype(jnp.float32), 0.0)
    out_ref[...] = jnp.broadcast_to(jnp.sum(kept, axis=1, keepdims=True), out_ref.shape).astype(out_ref.dtype)


def diagonal(gram, core, fine=128):
    width = gram.shape[0]
    tiles = width // fine
    return pl.pallas_call(
        diag_kernel,
        grid_spec=pltpu.PrefetchScalarGridSpec(
            num_scalar_prefetch=1,
            grid=(tiles,),
            in_specs=[pl.BlockSpec((fine, fine), lambda i, s: (i, s[0] * tiles + i))],
            out_specs=pl.BlockSpec((fine, fine), lambda i, s: (i, 0)),
        ),
        out_shape=jax.ShapeDtypeStruct((width, fine), gram.dtype),
        compiler_params=pltpu.CompilerParams(dimension_semantics=("arbitrary",)),
    )(core.reshape(1), gram)


def fetch(source, target, sem):
    copy = pltpu.make_async_copy(source, target, sem)
    copy.start()
    return copy


def step_kernel(t_ref, s_ref, lam_ref, act_ref, pen, diag, beta, corr, acc, *rest, tile, rounds):
    got, (step, pay), rest = rest[:rounds], rest[rounds : rounds + 2], rest[rounds + 2 :]
    pen_v, diag_v, beta_v, corr_v, acc_v, got_v, out_v, in_sems, out_sems = rest
    field = lambda name: at(t_ref, s_ref, name)
    width = out_v.shape[0]
    parts = [pl.ds(i * tile, tile) for i in range(width // tile)]

    @pl.when(field(VISITED) == 1)
    def _():
        place = field(PLACE)
        waits = []
        for i, part in enumerate(parts):
            pairs = [(x.at[place, part], v.at[part]) for x, v in ((pen, pen_v), (diag, diag_v), (corr, corr_v), (acc, acc_v))]
            pairs.append((beta.at[field(SLOT), part], beta_v.at[part]))
            pairs += [(r.at[part], got_v.at[n, part]) for n, r in enumerate(got)]
            waits.append([fetch(x, v, in_sems.at[i, n]) for n, (x, v) in enumerate(pairs)])
        act = act_ref[field(BLOCK)]
        outs = []
        for i, part in enumerate(parts):
            for copy in waits[i]:
                copy.wait()
            beta_old, diag_now = beta_v[part], diag_v[part][:, :1].astype(jnp.float32)
            grad = corr_v[part] - acc_v[part]
            for n in range(rounds):
                grad = grad - got_v[n, part].astype(jnp.float32)
            shifted = diag_now * beta_old + grad
            size = jnp.maximum(jnp.abs(shifted) - lam_ref[...] * pen_v[part][:, :1], 0.0) / diag_now
            beta_new = jnp.where(shifted < 0.0, -size, size)
            out_v[part] = jnp.where(act == 1, beta_new - beta_old, 0.0).astype(jnp.bfloat16)
            outs += [fetch(out_v.at[part], o.at[part], out_sems.at[i, n]) for n, o in enumerate((step, pay))]
        for copy in outs:
            copy.wait()

    @pl.when((field(VISITED) == 0) & (field(SENDS) == 1))
    def _():
        waits = [fetch(acc.at[field(NEXT), part], acc_v.at[part], in_sems.at[i, 0]) for i, part in enumerate(parts)]
        outs = []
        for i, part in enumerate(parts):
            waits[i].wait()
            out_v[part] = acc_v[part].astype(jnp.bfloat16)
            outs.append(fetch(out_v.at[part], pay.at[part], out_sems.at[i, 0]))
        for copy in outs:
            copy.wait()


def soft_step(turn, table, lam, act, pen, diag, beta, corr, acc, got, tile=512):
    _, width, resp = beta.shape
    fine, rounds = pen.shape[-1], len(got)
    whole, anywhere = pl.BlockSpec(memory_space=pltpu.VMEM), pl.BlockSpec(memory_space=pl.ANY)
    parts = width // tile
    return pl.pallas_call(
        functools.partial(step_kernel, tile=tile, rounds=rounds),
        grid_spec=pltpu.PrefetchScalarGridSpec(
            num_scalar_prefetch=2,
            in_specs=[whole, whole] + [anywhere] * (5 + rounds),
            out_specs=[anywhere, anywhere],
            scratch_shapes=[
                pltpu.VMEM((width, fine), pen.dtype),
                pltpu.VMEM((width, fine), diag.dtype),
                pltpu.VMEM((width, resp), jnp.float32),
                pltpu.VMEM((width, resp), jnp.float32),
                pltpu.VMEM((width, resp), jnp.float32),
                pltpu.VMEM((rounds, width, resp), jnp.bfloat16),
                pltpu.VMEM((width, resp), jnp.bfloat16),
                pltpu.SemaphoreType.DMA((parts, 5 + rounds)),
                pltpu.SemaphoreType.DMA((parts, 2)),
            ],
        ),
        out_shape=[jax.ShapeDtypeStruct((width, resp), jnp.bfloat16)] * 2,
        compiler_params=pltpu.CompilerParams(vmem_limit_bytes=24 << 20),
        cost_estimate=pl.CostEstimate(flops=20 * resp * width, bytes_accessed=26 * resp * width, transcendentals=0),
    )(turn, table, lam, act, pen, diag, beta, corr, acc, *got)


def gram_tile(own, g_own, g_sib, first_row, first_col, target, sem, start):
    rows, cols = target.shape
    where = (pl.ds(pl.multiple_of(first_row, rows), rows), pl.ds(pl.multiple_of(first_col, cols), cols))
    if not start:
        pltpu.make_async_copy(g_own.at[where], target, sem).wait()
        return

    @pl.when(own == 1)
    def _():
        pltpu.make_async_copy(g_own.at[where], target, sem).start()

    @pl.when(own == 0)
    def _():
        pltpu.make_async_copy(g_sib.at[where], target, sem).start()


def add_block(own, g_own, g_sib, slot, x_v, tiles_v, sems, store):
    _, tile, width = tiles_v.shape
    count = width // tile
    move = lambda i, start: gram_tile(
        own, g_own, g_sib, i * tile, slot * width, tiles_v.at[i % 2], sems.at[i % 2], start
    )

    def body(i, _):
        @pl.when(i + 1 < count)
        def _():
            move(i + 1, True)

        move(i, False)
        change = jnp.dot(tiles_v[i % 2], x_v[...], preferred_element_type=jnp.float32)
        store(pl.ds(pl.multiple_of(i * tile, tile), tile), change.astype(jnp.bfloat16).astype(jnp.float32))
        return 0

    lax.fori_loop(0, count, body, 0)


def relay_kernel(t_ref, s_ref, x, step, g_own, g_sib, acc, send, x_v, acc_v, out_v, tiles_v, sems, tile_sems):
    field = lambda name: at(t_ref, s_ref, name)

    @pl.when(field(RELAYS) == 1)
    def _():
        own, slot = flag(field(NEXT) == 0), field(SLOT)
        gram_tile(own, g_own, g_sib, 0, slot * tiles_v.shape[2], tiles_v.at[0], tile_sems.at[0], True)
        waits = [fetch(x, x_v, sems.at[0]), fetch(acc.at[field(NEXT)], acc_v, sems.at[1])]
        for copy in waits:
            copy.wait()

        def store(part, change):
            out_v[part] = (acc_v[part] + change).astype(jnp.bfloat16)

        add_block(own, g_own, g_sib, slot, x_v, tiles_v, tile_sems, store)
        fetch(out_v, send, sems.at[2]).wait()

    @pl.when((field(RELAYS) == 0) & (field(VISITED) == 1))
    def _():
        fetch(step, send, sems.at[3]).wait()


def relay(turn, table, x, step, g_own, g_sib, acc, tile=1024):
    width, resp = x.shape
    anywhere = pl.BlockSpec(memory_space=pl.ANY)
    return pl.pallas_call(
        relay_kernel,
        grid_spec=pltpu.PrefetchScalarGridSpec(
            num_scalar_prefetch=2,
            in_specs=[anywhere] * 5,
            out_specs=anywhere,
            scratch_shapes=[
                pltpu.VMEM((width, resp), jnp.bfloat16),
                pltpu.VMEM((width, resp), jnp.float32),
                pltpu.VMEM((width, resp), jnp.bfloat16),
                pltpu.VMEM((2, tile, width), jnp.bfloat16),
                pltpu.SemaphoreType.DMA((4,)),
                pltpu.SemaphoreType.DMA((2,)),
            ],
        ),
        out_shape=jax.ShapeDtypeStruct((width, resp), jnp.bfloat16),
        compiler_params=pltpu.CompilerParams(vmem_limit_bytes=16 << 20),
        cost_estimate=pl.CostEstimate(
            flops=2 * resp * width * width, bytes_accessed=2 * width * width, transcendentals=0
        ),
    )(turn, table, x, step, g_own, g_sib, acc)


def update_kernel(t_ref, s_ref, g_own, g_sib, acc_in, moved_in, *rest):
    *arrived, acc, moved, x_v, acc_v, tiles_v, sems, tile_sems, out_sems = rest
    field = lambda name: at(t_ref, s_ref, name)

    @pl.when(field(LINE) == 1)
    def _():
        slot = field(SLOT)
        start = lambda j: gram_tile(
            jnp.int32(1 - j), g_own, g_sib, 0, slot * tiles_v.shape[2], tiles_v.at[0], tile_sems.at[0], True
        )
        start(0)
        sums = fetch(acc_in, acc_v, sems.at[0])
        for n, r in enumerate(arrived):

            @pl.when(field(HOLDS) == n)
            def _():
                fetch(r, x_v, sems.at[1]).wait()

        kept = fetch(x_v, moved.at[slot], sems.at[2])
        sums.wait()
        outs = []
        for j in range(2):

            def store(part, change):
                acc_v[j, part] = acc_v[j, part] + change

            if j:
                start(1)
            add_block(jnp.int32(1 - j), g_own, g_sib, slot, x_v, tiles_v, tile_sems, store)
            outs.append(fetch(acc_v.at[j], acc.at[j], out_sems.at[j]))
        kept.wait()
        for copy in outs:
            copy.wait()


def update(turn, table, g_own, g_sib, acc, moved, arrived, tile=1024):
    _, width, resp = acc.shape
    anywhere = pl.BlockSpec(memory_space=pl.ANY)
    return pl.pallas_call(
        update_kernel,
        grid_spec=pltpu.PrefetchScalarGridSpec(
            num_scalar_prefetch=2,
            in_specs=[anywhere] * (4 + len(arrived)),
            out_specs=[anywhere, anywhere],
            scratch_shapes=[
                pltpu.VMEM((width, resp), jnp.bfloat16),
                pltpu.VMEM((2, width, resp), jnp.float32),
                pltpu.VMEM((2, tile, width), jnp.bfloat16),
                pltpu.SemaphoreType.DMA((3,)),
                pltpu.SemaphoreType.DMA((2,)),
                pltpu.SemaphoreType.DMA((2,)),
            ],
        ),
        out_shape=[jax.ShapeDtypeStruct(acc.shape, acc.dtype), jax.ShapeDtypeStruct(moved.shape, moved.dtype)],
        input_output_aliases={4: 0, 5: 1},
        compiler_params=pltpu.CompilerParams(vmem_limit_bytes=16 << 20),
        cost_estimate=pl.CostEstimate(
            flops=4 * resp * width * width, bytes_accessed=4 * width * width, transcendentals=0
        ),
    )(turn, table, g_own, g_sib, acc, moved, *arrived)


def start_kernel(k_ref, beta_ref, half_ref, flat_ref):
    resp = half_ref.shape[1]
    for lam in range(2):

        @pl.when(k_ref[0] == lam)
        def _():
            half_ref[...] = beta_ref[:, lam, :]

        flat_ref[:, lam * resp : (lam + 1) * resp] = beta_ref[:, lam, :].astype(flat_ref.dtype)


def start_beta(core, beta, tile=512):
    rows, lams, resp = beta.shape
    return pl.pallas_call(
        start_kernel,
        grid_spec=pltpu.PrefetchScalarGridSpec(
            num_scalar_prefetch=1,
            grid=(rows // tile,),
            in_specs=[pl.BlockSpec((tile, lams, resp), lambda i, k: (i, 0, 0))],
            out_specs=[
                pl.BlockSpec((tile, resp), lambda i, k: (i, 0)),
                pl.BlockSpec((tile, lams * resp), lambda i, k: (i, 0)),
            ],
        ),
        out_shape=[
            jax.ShapeDtypeStruct((rows, resp), beta.dtype),
            jax.ShapeDtypeStruct((rows, lams * resp), jnp.bfloat16),
        ],
    )(core, beta)


def join_kernel(k_ref, mine_ref, other_ref, *rest):
    *base, out_ref = rest
    for lam in range(2):
        value = jnp.where(k_ref[0] == lam, mine_ref[...], other_ref[...]).astype(out_ref.dtype)
        out_ref[:, lam, :] = value + base[0][:, lam, :] if base else value


def join(core, mine, other, base=(), tile=512):
    rows, resp = mine.shape
    flat = pl.BlockSpec((tile, resp), lambda i, k: (i, 0))
    deep = pl.BlockSpec((tile, 2, resp), lambda i, k: (i, 0, 0))
    return pl.pallas_call(
        join_kernel,
        grid_spec=pltpu.PrefetchScalarGridSpec(
            num_scalar_prefetch=1, grid=(rows // tile,), in_specs=[flat, flat] + [deep] * len(base), out_specs=deep
        ),
        out_shape=jax.ShapeDtypeStruct((rows, 2, resp), jnp.float32),
        cost_estimate=pl.CostEstimate(flops=4 * rows * resp, bytes_accessed=20 * rows * resp, transcendentals=0),
    )(core, mine, other, *base)


def routes(p, pn, planes, lines):
    rest_q = [c for c in range(lines) if c not in (p, pn)]
    rest_z = sorted([c for c in range(planes) if c not in (p, pn)], key=lambda c: abs(c - p) - abs(c - pn))
    if p == pn:
        return [([((p, p), (c, p)), ((p, c), (p, p))], c, p) for c in rest_z]
    first = ([((p, p), (pn, p))] + [((pn, c), (pn, pn)) for c in rest_q[:1]], pn, p)
    last = ([((pn, p), (pn, pn))] + [((p, p), (c, p)) for c in rest_z[:1]], rest_z[0] if rest_z else pn, p)
    between = []
    for line, plane in zip(rest_q[1:], rest_z[1:]):
        source = p if abs(plane - p) < abs(plane - pn) else pn
        between.append(([((source, p), (plane, p)), ((pn, line), (pn, pn))], plane, source))
    return [first, *between, last]


def per_device(planes, lines, gram, corr, beta_start, lambdas, penalty, strong, active, order):
    width = corr.shape[0]
    lam_count, phenos = beta_start.shape[1:]
    cols = lam_count * phenos
    half = cols // 2
    row = lax.axis_index("row")
    z, k, q = row // 2, row % 2, lax.axis_index("col")
    swap = [(r * lines + c, (r ^ 1) * lines + c) for r in range(2 * planes) for c in range(lines)]
    permute = lambda x, pairs: lax.ppermute(x, ("row", "col"), pairs)
    pair_of = lambda mine: jnp.stack([mine, permute(mine, swap)])
    core = k.reshape(1)

    def gather_col(x):
        return lax.all_to_all(jnp.broadcast_to(x[None], (lines, *x.shape)), "col", 0, 0)

    g_sib = permute(gram, swap)

    beta_half, flat = start_beta(core, beta_start)
    product = jnp.dot(gram, flat, preferred_element_type=jnp.float32)
    other = permute(lax.dynamic_slice_in_dim(product, (1 - k) * half, half, 1), swap)
    shares = jnp.stack([lax.dynamic_slice_in_dim(product, k * half, half, 1), other])

    fine = 128
    wanted = penalty.reshape(-1, fine)[strong // fine]
    chosen = lax.broadcasted_iota(jnp.int32, wanted.shape, 1) == (strong % fine)[:, None]
    pen_own = jnp.broadcast_to(jnp.sum(jnp.where(chosen, wanted, 0.0), axis=1, keepdims=True), wanted.shape)
    diag_own = diagonal(gram, k, fine)
    pen, diag = pair_of(pen_own), pair_of(diag_own)

    corr = pair_of(corr)
    beta0 = beta_half.reshape(2, width, half)
    lam = lax.dynamic_slice_in_dim(jnp.repeat(lambdas, phenos), k * half, half)[None, :]
    act = lax.dynamic_slice_in_dim(jnp.repeat(active.T, phenos, axis=1), k * half, half, 1)[:, None, :]

    holds = np.zeros((planes, planes, planes), np.int32)
    for p in range(planes):
        for pn in range(planes):
            for n, (_, plane, _) in enumerate(routes(p, pn, planes, lines)):
                holds[p, pn, plane] = n + 1
            holds[p, pn, p] = 0
    after = jnp.concatenate([order, order[-1:]])
    order = jnp.concatenate([order[:1], order])
    real = flag(jnp.arange(order.shape[0]) > 0)
    pair, pair_n, slot_n = order // 2, after // 2, after % 2
    held = lax.dynamic_index_in_dim(jnp.asarray(holds), z, 2, keepdims=False)[pair, pair_n]
    line = flag(q == pair) * real
    table = jnp.stack(
        [
            order % 2,
            order,
            (order % 2) ^ k,
            flag(z == pair) * line,
            line,
            held,
            flag((z == pair_n) & (pair != pair_n)) * line,
            slot_n ^ k,
            flag(z == pair_n),
        ],
        axis=1,
    ).reshape(-1)
    which = pair * planes + pair_n

    def branch(p, pn):
        plan = routes(p, pn, planes, lines)
        send = lambda payload, flows: permute(payload, device_pairs(flows, planes, lines))

        def run(operands):
            turn, step, pay, acc = operands
            if p == pn:
                return tuple(send(pay, flows) for flows, _, _ in plan)
            at_pn = (z == pn) & (q == p)
            first = send(pay, plan[0][0])
            out = relay(turn, table, first, step, gram, g_sib, acc)
            late, late_pay, out = lax.optimization_barrier((first, pay, out))
            between = [
                send(pay if source == p else jnp.where(at_pn, late, late_pay), flows) for flows, _, source in plan[1:-1]
            ]
            return (first, *between, send(out, plan[-1][0]))

        return run

    branches = [branch(p, pn) for p in range(planes) for pn in range(planes)]

    def visit(count, carry):
        acc, moved, got = carry
        turn = count.reshape(1)
        step, pay = soft_step(turn, table, lam, act, pen, diag, beta0, corr, acc, got)
        got = lax.switch(which[count], branches, (turn, step, pay, acc))
        acc, moved = update(turn, table, gram, g_sib, acc, moved, (step, *got))
        return acc, moved, got

    empty = jnp.zeros((2, width, half), jnp.bfloat16)
    carry = (shares, empty, (empty[0],) * (planes - 1))
    acc, moved, _ = lax.fori_loop(0, order.shape[0], visit, carry)

    part = width // lines
    acc, moved_other = lax.optimization_barrier((acc, permute(moved, swap)))
    share = lax.all_to_all(acc.reshape(2, lines, part, half).swapaxes(0, 1), "col", 0, 0)
    beta = join(
        core, moved.reshape(2 * width, half), moved_other.reshape(2 * width, half), (beta_start,)
    )
    share = lax.dynamic_slice_in_dim(corr, q * part, part, 1) - jnp.sum(share, axis=0)
    final = gather_col(share.astype(jnp.bfloat16))
    other = permute(final[:, 1].reshape(width, half), swap)
    return beta, join(core, final[:, 0].reshape(width, half), other)


def solution(mesh):
    planes, lines = mesh.shape["row"] // 2, mesh.shape["col"]
    in_specs = (P("row", "col"), P("row", None), P("col", None, None), P(), P(), P("row"), P(), P())
    out_specs = (P("col", None, None), P("row", None, None))
    return jax.shard_map(
        functools.partial(per_device, planes, lines),
        mesh=mesh, in_specs=in_specs, out_specs=out_specs, check_vma=False,
    )
```

```python
import functools

import jax
import jax.numpy as jnp
import numpy as np
from jax import lax
from jax.experimental import pallas as pl
from jax.experimental.pallas import tpu as pltpu
from jax.sharding import PartitionSpec as P

FIELDS = 9
SLOT, BLOCK, PLACE, VISITED, LINE, HOLDS, RELAYS, NEXT, SENDS = range(FIELDS)


def flag(value):
    return value.astype(jnp.int32)


def at(turn, table, field):
    return table[turn[0] * FIELDS + field]


def device_pairs(flows, planes, lines):
    nxt = dict(flows)
    for start in [a for a in nxt if a not in nxt.values()]:
        end = start
        while end in nxt:
            end = nxt[end]
        nxt[end] = start
    pairs = []
    for z in range(planes):
        for q in range(lines):
            for k in range(2):
                to_z, to_q = nxt.get((z, q), (z, q))
                to_k = k if (z, q) in nxt else 1 - k
                pairs.append(((2 * z + k) * lines + q, (2 * to_z + to_k) * lines + to_q))
    return pairs


def diag_kernel(s_ref, block_ref, out_ref):
    rows = lax.broadcasted_iota(jnp.int32, block_ref.shape, 0)
    cols = lax.broadcasted_iota(jnp.int32, block_ref.shape, 1)
    kept = jnp.where(rows == cols, block_ref[...].astype(jnp.float32), 0.0)
    out_ref[...] = jnp.broadcast_to(jnp.sum(kept, axis=1, keepdims=True), out_ref.shape).astype(out_ref.dtype)


def diagonal(gram, core, lanes, fine=512):
    width = gram.shape[0]
    tiles = width // fine
    return pl.pallas_call(
        diag_kernel,
        grid_spec=pltpu.PrefetchScalarGridSpec(
            num_scalar_prefetch=1,
            grid=(tiles,),
            in_specs=[pl.BlockSpec((fine, fine), lambda i, s: (i, s[0] * tiles + i))],
            out_specs=pl.BlockSpec((fine, lanes), lambda i, s: (i, 0)),
        ),
        out_shape=jax.ShapeDtypeStruct((width, lanes), gram.dtype),
        compiler_params=pltpu.CompilerParams(dimension_semantics=("arbitrary",)),
    )(core.reshape(1), gram)


def fetch(source, target, sem):
    copy = pltpu.make_async_copy(source, target, sem)
    copy.start()
    return copy


def step_kernel(t_ref, s_ref, lam_ref, act_ref, pen, diag, beta, corr, acc, *rest, tile, rounds):
    got, (step, pay), rest = rest[:rounds], rest[rounds : rounds + 2], rest[rounds + 2 :]
    pen_v, diag_v, beta_v, corr_v, acc_v, got_v, out_v, in_sems, out_sems = rest
    field = lambda name: at(t_ref, s_ref, name)
    width = out_v.shape[0]
    parts = [pl.ds(i * tile, tile) for i in range(width // tile)]

    @pl.when(field(VISITED) == 1)
    def _():
        place = field(PLACE)
        waits = []
        for i, part in enumerate(parts):
            pairs = [(x.at[place, part], v.at[part]) for x, v in ((pen, pen_v), (diag, diag_v), (corr, corr_v), (acc, acc_v))]
            pairs.append((beta.at[field(SLOT), part], beta_v.at[part]))
            pairs += [(r.at[part], got_v.at[n, part]) for n, r in enumerate(got)]
            waits.append([fetch(x, v, in_sems.at[i, n]) for n, (x, v) in enumerate(pairs)])
        act = act_ref[field(BLOCK)]
        outs = []
        for i, part in enumerate(parts):
            for copy in waits[i]:
                copy.wait()
            beta_old, diag_now = beta_v[part], diag_v[part][:, :1].astype(jnp.float32)
            grad = corr_v[part] - acc_v[part]
            for n in range(rounds):
                grad = grad - got_v[n, part].astype(jnp.float32)
            shifted = diag_now * beta_old + grad
            size = jnp.maximum(jnp.abs(shifted) - lam_ref[...] * pen_v[part][:, :1], 0.0) / diag_now
            beta_new = jnp.where(shifted < 0.0, -size, size)
            out_v[part] = jnp.where(act == 1, beta_new - beta_old, 0.0).astype(jnp.bfloat16)
            outs += [fetch(out_v.at[part], o.at[part], out_sems.at[i, n]) for n, o in enumerate((step, pay))]
        for copy in outs:
            copy.wait()

    @pl.when((field(VISITED) == 0) & (field(SENDS) == 1))
    def _():
        waits = [fetch(acc.at[field(NEXT), part], acc_v.at[part], in_sems.at[i, 0]) for i, part in enumerate(parts)]
        outs = []
        for i, part in enumerate(parts):
            waits[i].wait()
            out_v[part] = acc_v[part].astype(jnp.bfloat16)
            outs.append(fetch(out_v.at[part], pay.at[part], out_sems.at[i, 0]))
        for copy in outs:
            copy.wait()


def soft_step(turn, table, lam, act, pen, diag, beta, corr, acc, got, tile=512):
    _, width, resp = beta.shape
    fine, rounds = pen.shape[-1], len(got)
    whole, anywhere = pl.BlockSpec(memory_space=pltpu.VMEM), pl.BlockSpec(memory_space=pl.ANY)
    parts = width // tile
    return pl.pallas_call(
        functools.partial(step_kernel, tile=tile, rounds=rounds),
        grid_spec=pltpu.PrefetchScalarGridSpec(
            num_scalar_prefetch=2,
            in_specs=[whole, whole] + [anywhere] * (5 + rounds),
            out_specs=[anywhere, anywhere],
            scratch_shapes=[
                pltpu.VMEM((width, fine), pen.dtype),
                pltpu.VMEM((width, fine), diag.dtype),
                pltpu.VMEM((width, resp), jnp.float32),
                pltpu.VMEM((width, resp), jnp.float32),
                pltpu.VMEM((width, resp), jnp.float32),
                pltpu.VMEM((rounds, width, resp), jnp.bfloat16),
                pltpu.VMEM((width, resp), jnp.bfloat16),
                pltpu.SemaphoreType.DMA((parts, 5 + rounds)),
                pltpu.SemaphoreType.DMA((parts, 2)),
            ],
        ),
        out_shape=[jax.ShapeDtypeStruct((width, resp), jnp.bfloat16)] * 2,
        compiler_params=pltpu.CompilerParams(vmem_limit_bytes=24 << 20),
        cost_estimate=pl.CostEstimate(flops=20 * resp * width, bytes_accessed=26 * resp * width, transcendentals=0),
    )(turn, table, lam, act, pen, diag, beta, corr, acc, *got)


def gram_tile(own, g_own, g_sib, first_row, first_col, target, sem, start):
    rows, cols = target.shape
    where = (pl.ds(pl.multiple_of(first_row, rows), rows), pl.ds(pl.multiple_of(first_col, cols), cols))
    if not start:
        pltpu.make_async_copy(g_own.at[where], target, sem).wait()
        return

    @pl.when(own == 1)
    def _():
        pltpu.make_async_copy(g_own.at[where], target, sem).start()

    @pl.when(own == 0)
    def _():
        pltpu.make_async_copy(g_sib.at[where], target, sem).start()


def add_block(own, g_own, g_sib, slot, x_v, tiles_v, sems, store):
    _, tile, width = tiles_v.shape
    count = width // tile
    move = lambda i, start: gram_tile(
        own, g_own, g_sib, i * tile, slot * width, tiles_v.at[i % 2], sems.at[i % 2], start
    )

    def body(i, _):
        @pl.when(i + 1 < count)
        def _():
            move(i + 1, True)

        move(i, False)
        change = jnp.dot(tiles_v[i % 2], x_v[...], preferred_element_type=jnp.float32)
        store(pl.ds(pl.multiple_of(i * tile, tile), tile), change.astype(jnp.bfloat16).astype(jnp.float32))
        return 0

    lax.fori_loop(0, count, body, 0)


def relay_kernel(t_ref, s_ref, x, step, pay, g_own, g_sib, acc, send, late, x_v, acc_v, out_v, tiles_v, sems, tile_sems):
    field = lambda name: at(t_ref, s_ref, name)

    @pl.when(field(RELAYS) == 1)
    def _():
        own, slot = flag(field(NEXT) == 0), field(SLOT)
        gram_tile(own, g_own, g_sib, 0, slot * tiles_v.shape[2], tiles_v.at[0], tile_sems.at[0], True)
        waits = [fetch(x, x_v, sems.at[0]), fetch(acc.at[field(NEXT)], acc_v, sems.at[1])]
        for copy in waits:
            copy.wait()

        def store(part, change):
            out_v[part] = (acc_v[part] + change).astype(jnp.bfloat16)

        onward = fetch(x_v, late, sems.at[4])
        add_block(own, g_own, g_sib, slot, x_v, tiles_v, tile_sems, store)
        fetch(out_v, send, sems.at[2]).wait()
        onward.wait()

    @pl.when((field(RELAYS) == 0) & (field(VISITED) == 1))
    def _():
        fetch(step, send, sems.at[3]).wait()

    @pl.when((field(RELAYS) == 0) & ((field(VISITED) == 1) | (field(SENDS) == 1)))
    def _():
        fetch(pay, late, sems.at[4]).wait()


def relay(turn, table, x, step, pay, g_own, g_sib, acc, tile=1024):
    width, resp = x.shape
    anywhere = pl.BlockSpec(memory_space=pl.ANY)
    return pl.pallas_call(
        relay_kernel,
        grid_spec=pltpu.PrefetchScalarGridSpec(
            num_scalar_prefetch=2,
            in_specs=[anywhere] * 6,
            out_specs=[anywhere, anywhere],
            scratch_shapes=[
                pltpu.VMEM((width, resp), jnp.bfloat16),
                pltpu.VMEM((width, resp), jnp.float32),
                pltpu.VMEM((width, resp), jnp.bfloat16),
                pltpu.VMEM((2, tile, width), jnp.bfloat16),
                pltpu.SemaphoreType.DMA((5,)),
                pltpu.SemaphoreType.DMA((2,)),
            ],
        ),
        out_shape=[jax.ShapeDtypeStruct((width, resp), jnp.bfloat16)] * 2,
        compiler_params=pltpu.CompilerParams(vmem_limit_bytes=16 << 20),
        cost_estimate=pl.CostEstimate(
            flops=2 * resp * width * width, bytes_accessed=2 * width * width, transcendentals=0
        ),
    )(turn, table, x, step, pay, g_own, g_sib, acc)


def update_kernel(t_ref, s_ref, g_own, g_sib, acc_in, moved_in, *rest):
    *arrived, acc, moved, x_v, acc_v, tiles_v, sems, tile_sems, out_sems = rest
    field = lambda name: at(t_ref, s_ref, name)

    @pl.when(field(LINE) == 1)
    def _():
        slot = field(SLOT)
        start = lambda j: gram_tile(
            jnp.int32(1 - j), g_own, g_sib, 0, slot * tiles_v.shape[2], tiles_v.at[0], tile_sems.at[0], True
        )
        start(0)
        sums = fetch(acc_in, acc_v, sems.at[0])
        for n, r in enumerate(arrived):

            @pl.when(field(HOLDS) == n)
            def _():
                fetch(r, x_v, sems.at[1]).wait()

        kept = fetch(x_v, moved.at[slot], sems.at[2])
        sums.wait()
        outs = []
        for j in range(2):

            def store(part, change):
                acc_v[j, part] = acc_v[j, part] + change

            if j:
                start(1)
            add_block(jnp.int32(1 - j), g_own, g_sib, slot, x_v, tiles_v, tile_sems, store)
            outs.append(fetch(acc_v.at[j], acc.at[j], out_sems.at[j]))
        kept.wait()
        for copy in outs:
            copy.wait()


def update(turn, table, g_own, g_sib, acc, moved, arrived, tile=1024):
    _, width, resp = acc.shape
    anywhere = pl.BlockSpec(memory_space=pl.ANY)
    return pl.pallas_call(
        update_kernel,
        grid_spec=pltpu.PrefetchScalarGridSpec(
            num_scalar_prefetch=2,
            in_specs=[anywhere] * (4 + len(arrived)),
            out_specs=[anywhere, anywhere],
            scratch_shapes=[
                pltpu.VMEM((width, resp), jnp.bfloat16),
                pltpu.VMEM((2, width, resp), jnp.float32),
                pltpu.VMEM((2, tile, width), jnp.bfloat16),
                pltpu.SemaphoreType.DMA((3,)),
                pltpu.SemaphoreType.DMA((2,)),
                pltpu.SemaphoreType.DMA((2,)),
            ],
        ),
        out_shape=[jax.ShapeDtypeStruct(acc.shape, acc.dtype), jax.ShapeDtypeStruct(moved.shape, moved.dtype)],
        input_output_aliases={4: 0, 5: 1},
        compiler_params=pltpu.CompilerParams(vmem_limit_bytes=16 << 20),
        cost_estimate=pl.CostEstimate(
            flops=4 * resp * width * width, bytes_accessed=4 * width * width, transcendentals=0
        ),
    )(turn, table, g_own, g_sib, acc, moved, *arrived)


def start_kernel(k_ref, beta_ref, half_ref, flat_ref):
    resp = half_ref.shape[1]
    for lam in range(2):

        @pl.when(k_ref[0] == lam)
        def _():
            half_ref[...] = beta_ref[:, lam, :]

        flat_ref[:, lam * resp : (lam + 1) * resp] = beta_ref[:, lam, :].astype(flat_ref.dtype)


def start_beta(core, beta, tile=512):
    rows, lams, resp = beta.shape
    return pl.pallas_call(
        start_kernel,
        grid_spec=pltpu.PrefetchScalarGridSpec(
            num_scalar_prefetch=1,
            grid=(rows // tile,),
            in_specs=[pl.BlockSpec((tile, lams, resp), lambda i, k: (i, 0, 0))],
            out_specs=[
                pl.BlockSpec((tile, resp), lambda i, k: (i, 0)),
                pl.BlockSpec((tile, lams * resp), lambda i, k: (i, 0)),
            ],
        ),
        out_shape=[
            jax.ShapeDtypeStruct((rows, resp), beta.dtype),
            jax.ShapeDtypeStruct((rows, lams * resp), jnp.bfloat16),
        ],
    )(core, beta)


def join_kernel(k_ref, mine_ref, other_ref, *rest):
    *base, out_ref = rest
    for lam in range(2):
        value = jnp.where(k_ref[0] == lam, mine_ref[...], other_ref[...]).astype(out_ref.dtype)
        out_ref[:, lam, :] = value + base[0][:, lam, :] if base else value


def join(core, mine, other, base=(), tile=512):
    rows, resp = mine.shape
    flat = pl.BlockSpec((tile, resp), lambda i, k: (i, 0))
    deep = pl.BlockSpec((tile, 2, resp), lambda i, k: (i, 0, 0))
    return pl.pallas_call(
        join_kernel,
        grid_spec=pltpu.PrefetchScalarGridSpec(
            num_scalar_prefetch=1, grid=(rows // tile,), in_specs=[flat, flat] + [deep] * len(base), out_specs=deep
        ),
        out_shape=jax.ShapeDtypeStruct((rows, 2, resp), jnp.float32),
        cost_estimate=pl.CostEstimate(flops=4 * rows * resp, bytes_accessed=20 * rows * resp, transcendentals=0),
    )(core, mine, other, *base)


def routes(p, pn, planes, lines):
    rest_q = sorted([c for c in range(lines) if c not in (p, pn)], key=lambda c: c == pn ^ 1)
    rest_z = sorted([c for c in range(planes) if c not in (p, pn)], key=lambda c: abs(c - p) - abs(c - pn))
    if p == pn:
        return [([((p, p), (c, p)), ((p, c), (p, p))], c, p) for c in rest_z]
    first = ([((p, p), (pn, p))] + [((pn, c), (pn, pn)) for c in rest_q[:1]], pn, p)
    last = ([((pn, p), (pn, pn))] + [((p, p), (c, p)) for c in rest_z[:1]], rest_z[0] if rest_z else pn, p)
    between = []
    for line, plane in zip(rest_q[1:], rest_z[1:]):
        source = p if abs(plane - p) < abs(plane - pn) else pn
        between.append(([((source, p), (plane, p)), ((pn, line), (pn, pn))], plane, source))
    return [first, *between, last]


def per_device(planes, lines, gram, corr, beta_start, lambdas, penalty, strong, active, order):
    width = corr.shape[0]
    lam_count, phenos = beta_start.shape[1:]
    cols = lam_count * phenos
    half = cols // 2
    row = lax.axis_index("row")
    z, k, q = row // 2, row % 2, lax.axis_index("col")
    swap = [(r * lines + c, (r ^ 1) * lines + c) for r in range(2 * planes) for c in range(lines)]
    permute = lambda x, pairs: lax.ppermute(x, ("row", "col"), pairs)
    pair_of = lambda mine: jnp.stack([mine, permute(mine, swap)])
    core = k.reshape(1)

    def gather_col(x):
        return lax.all_to_all(jnp.broadcast_to(x[None], (lines, *x.shape)), "col", 0, 0)

    g_sib = permute(gram, swap)

    beta_half, flat = start_beta(core, beta_start)
    product = jnp.dot(gram, flat, preferred_element_type=jnp.float32)
    other = permute(lax.dynamic_slice_in_dim(product, (1 - k) * half, half, 1), swap)
    shares = jnp.stack([lax.dynamic_slice_in_dim(product, k * half, half, 1), other])

    fine = 128
    wanted = penalty.reshape(-1, fine)[strong // fine]
    chosen = lax.broadcasted_iota(jnp.int32, wanted.shape, 1) == (strong % fine)[:, None]
    pen_own = jnp.broadcast_to(jnp.sum(jnp.where(chosen, wanted, 0.0), axis=1, keepdims=True), wanted.shape)
    diag_own = diagonal(gram, k, fine)
    pen, diag = pair_of(pen_own), pair_of(diag_own)

    corr = pair_of(corr)
    beta0 = beta_half.reshape(2, width, half)
    lam = lax.dynamic_slice_in_dim(jnp.repeat(lambdas, phenos), k * half, half)[None, :]
    act = lax.dynamic_slice_in_dim(jnp.repeat(active.T, phenos, axis=1), k * half, half, 1)[:, None, :]

    holds = np.zeros((planes, planes, planes), np.int32)
    for p in range(planes):
        for pn in range(planes):
            for n, (_, plane, _) in enumerate(routes(p, pn, planes, lines)):
                holds[p, pn, plane] = n + 1
            holds[p, pn, p] = 0
    after = jnp.concatenate([order[1:], order[-1:]])
    pair, pair_n, slot_n = order // 2, after // 2, after % 2
    held = lax.dynamic_index_in_dim(jnp.asarray(holds), z, 2, keepdims=False)[pair, pair_n]
    line = flag(q == pair)
    table = jnp.stack(
        [
            order % 2,
            order,
            (order % 2) ^ k,
            flag(z == pair) * line,
            line,
            held,
            flag((z == pair_n) & (pair != pair_n)) * line,
            slot_n ^ k,
            flag(z == pair_n),
        ],
        axis=1,
    ).reshape(-1)
    which = pair * planes + pair_n

    def branch(p, pn):
        plan = routes(p, pn, planes, lines)
        send = lambda payload, flows: permute(payload, device_pairs(flows, planes, lines))

        def run(operands):
            turn, step, pay, acc = operands
            if p == pn:
                return tuple(send(pay, flows) for flows, _, _ in plan)
            first = send(pay, plan[0][0])
            out, late = relay(turn, table, first, step, pay, gram, g_sib, acc)
            last = send(out, plan[-1][0])
            between = [send(pay if source == p else late, flows) for flows, _, source in plan[1:-1]]
            return (first, *between, last)

        return run

    branches = [branch(p, pn) for p in range(planes) for pn in range(planes)]

    def visit(count, carry):
        acc, moved, got = carry
        turn = count.reshape(1)
        step, pay = soft_step(turn, table, lam, act, pen, diag, beta0, corr, acc, got)
        got = lax.switch(which[count], branches, (turn, step, pay, acc))
        acc, moved = update(turn, table, gram, g_sib, acc, moved, (step, *got))
        return acc, moved, got

    empty = jnp.zeros((2, width, half), jnp.bfloat16)

    def opening(p):
        def run(payload):
            return tuple(
                permute(payload, device_pairs([((p, c), (p, p))], planes, lines)) for c in range(lines) if c != p
            )

        return run

    began = lax.dynamic_index_in_dim(shares, (order[0] % 2) ^ k, 0, keepdims=False).astype(jnp.bfloat16)
    carry = (shares, empty, lax.switch(order[0] // 2, [opening(p) for p in range(planes)], began))
    acc, moved, _ = lax.fori_loop(0, order.shape[0], visit, carry)

    part = width // lines
    acc, moved_other = lax.optimization_barrier((acc, permute(moved, swap)))
    share = lax.all_to_all(acc.reshape(2, lines, part, half).swapaxes(0, 1), "col", 0, 0)
    beta = join(
        core, moved.reshape(2 * width, half), moved_other.reshape(2 * width, half), (beta_start,)
    )
    share, beta = lax.optimization_barrier((share, beta))
    share = lax.dynamic_slice_in_dim(corr, q * part, part, 1) - jnp.sum(share, axis=0)
    final = gather_col(share.astype(jnp.bfloat16))
    other = permute(final[:, 1].reshape(width, half), swap)
    return beta, join(core, final[:, 0].reshape(width, half), other)


def solution(mesh):
    planes, lines = mesh.shape["row"] // 2, mesh.shape["col"]
    in_specs = (P("row", "col"), P("row", None), P("col", None, None), P(), P(), P("row"), P(), P())
    out_specs = (P("col", None, None), P("row", None, None))
    return jax.shard_map(
        functools.partial(per_device, planes, lines),
        mesh=mesh, in_specs=in_specs, out_specs=out_specs, check_vma=False,
    )
```
